768 devices in a mesh: ctx: 12 (over z), head: 64 (over x, y, core).
Axes of the slice: x: 4, y: 8, z: 12, core: 2. Of those that a mesh axis runs over, the one named last changes fastest.
Arguments:
- queries: bfloat16 [24576, 8192], P('ctx', 'head'), may hold values from -6 to 6
- keys: bfloat16 [24576, 8192], P('ctx', 'head'), may hold values from -0.5 to 0.5
- values: bfloat16 [24576, 8192], P('ctx', 'head'), may hold values from -24 to 24
- norm_gain: float32 [8192], P('head'), may hold values from 0.1 to 1.9
- out_grad: bfloat16 [24576, 8192], P('ctx', 'head'), may hold values from -6 to 6
Outputs:
- query_grad: bfloat16 [24576, 8192], P('ctx', 'head')
- key_grad: bfloat16 [24576, 8192], P('ctx', 'head')
- value_grad: bfloat16 [24576, 8192], P('ctx', 'head')
The draws below stay inside these ranges and needn't reach their ends.
All inputs are finite; a program needn't handle non-finite values.
Results may differ from the reference program's by a relative error of at most 0.005.
Values sent between devices are 32-bit elements; how exact they have to be, the bound alone decides.
A program may use at most 32 MiB of HBM per device.

```python
import jax
import jax.numpy as jnp
from jax import lax

HEAD_DIM = 128
GROUP = 512
HEADS = 64
D = 8192
TOKENS = 24576


def draw_values(key, part):
    width = HEADS * HEAD_DIM
    head_index = (jnp.arange(width) // HEAD_DIM).astype(jnp.float32)
    spread = 1.0 + 2.0 * head_index / max(HEADS - 1, 1)
    drawn = jax.random.normal(key, (TOKENS, width), jnp.float32) * spread[None, :]
    return jnp.clip(drawn, -24.0, 24.0).astype(jnp.bfloat16)


def shard_levels(own_key, extent, cuts, smallest, top_value):
    level = 1.0
    for axis_at, shards_of in cuts:
        draws = jax.random.uniform(jax.random.fold_in(jax.random.fold_in(own_key, 6), axis_at), (shards_of,), jnp.float32, smallest / len(cuts), top_value / len(cuts))
        level = level * jnp.repeat(jnp.exp(draws), extent[axis_at] // shards_of).reshape((-1,) + (1,) * (len(extent) - 1 - axis_at))
    return level


def noise(stream_key, extent, scale, bound, cuts=(), kind=jnp.bfloat16):
    values = scale * jax.random.normal(stream_key, extent, jnp.float32)
    if cuts:
        values = values * shard_levels(stream_key, extent, cuts, -0.22, 0.18)
    return jnp.clip(values, -bound, bound).astype(kind)


def setup_inputs(seed: int = 0) -> dict:
    streams_of = jax.random.split(jax.random.key(seed), 6)
    return {
        "queries": noise(streams_of[0], (TOKENS, D), 1.0, 6.0, ((0, 12), (1, 64))),
        "keys": noise(streams_of[1], (TOKENS, D), HEAD_DIM ** -0.5, 0.5, ((0, 12), (1, 64))),
        "values": draw_values(jax.random.fold_in(streams_of[5], 71), 0),
        "norm_gain": jnp.clip(1.0 + 0.18 * jax.random.normal(streams_of[3], (D,), jnp.float32), 0.1, 1.9),
        "out_grad": noise(streams_of[4], (TOKENS, D), 1.0, 6.0, ((0, 12), (1, 64))),
    }


HIGH = lax.Precision.HIGHEST

def heads_of(array, start):
    piece = lax.dynamic_slice_in_dim(array, start, GROUP, 0).astype(jnp.float32)
    return piece.reshape(GROUP, HEADS, HEAD_DIM).transpose(1, 0, 2)

def flat_of(piece):
    return piece.transpose(1, 0, 2).reshape(GROUP, HEADS * HEAD_DIM)

def reference(queries, keys, values, norm_gain, out_grad):
    blocks = TOKENS // GROUP
    causal = jnp.tril(jnp.ones((GROUP, GROUP), jnp.float32))
    gain = norm_gain.astype(jnp.float32).reshape(HEADS, 1, HEAD_DIM)
    width = HEADS * HEAD_DIM

    def forward(state, index):
        start = (index * GROUP).astype(jnp.int32)
        qpart = heads_of(queries, start)
        kpart = heads_of(keys, start)
        vpart = heads_of(values, start)
        upart = heads_of(out_grad, start) * gain
        scores = (jnp.einsum('hcd,hsd->hcs', qpart, kpart, precision=HIGH) * causal).astype(jnp.bfloat16).astype(jnp.float32)
        attended = jnp.einsum('hcs,hse->hce', scores, vpart, precision=HIGH) + jnp.einsum('hcd,hde->hce', qpart, state, precision=HIGH)
        power = lax.optimization_barrier(jnp.sum(attended * attended, axis=(0, 2))) / width
        cross = lax.optimization_barrier(jnp.sum(attended * upart, axis=(0, 2))) / width
        ratio = lax.rsqrt(power + 1e-06)
        agrad = (ratio[None, :, None] * upart - attended * (ratio ** 3 * cross)[None, :, None]).astype(jnp.bfloat16)
        agf = agrad.astype(jnp.float32)
        backflow = (jnp.einsum('hce,hse->hcs', agf, vpart, precision=HIGH) * causal).astype(jnp.bfloat16).astype(jnp.float32)
        qgrad = jnp.einsum('hcs,hsd->hcd', backflow, kpart, precision=HIGH) + jnp.einsum('hce,hde->hcd', agf, state, precision=HIGH)
        state = state + jnp.einsum('hsd,hse->hde', kpart, vpart, precision=HIGH)
        return (state, (flat_of(qgrad).astype(jnp.bfloat16), flat_of(agf).astype(jnp.bfloat16)))
    zero_state = jnp.zeros((HEADS, HEAD_DIM, HEAD_DIM), jnp.float32)
    order = jnp.arange(blocks, dtype=jnp.int32)
    _, (qgrads, agrads) = lax.scan(forward, zero_state, order)
    query_grad = qgrads.reshape(TOKENS, width)
    agrad_all = agrads.reshape(TOKENS, width)

    def backward(adjoint, index):
        start = (index * GROUP).astype(jnp.int32)
        qpart = heads_of(queries, start)
        kpart = heads_of(keys, start)
        vpart = heads_of(values, start)
        agf = heads_of(agrad_all, start)
        scores = (jnp.einsum('hcd,hsd->hcs', qpart, kpart, precision=HIGH) * causal).astype(jnp.bfloat16).astype(jnp.float32)
        backflow = (jnp.einsum('hce,hse->hcs', agf, vpart, precision=HIGH) * causal).astype(jnp.bfloat16).astype(jnp.float32)
        kgrad = jnp.einsum('hts,htd->hsd', backflow, qpart, precision=HIGH) + jnp.einsum('hse,hde->hsd', vpart, adjoint, precision=HIGH)
        vgrad = jnp.einsum('hts,hte->hse', scores, agf, precision=HIGH) + jnp.einsum('hsd,hde->hse', kpart, adjoint, precision=HIGH)
        adjoint = adjoint + jnp.einsum('htd,hte->hde', qpart, agf, precision=HIGH)
        return (adjoint, (flat_of(kgrad).astype(jnp.bfloat16), flat_of(vgrad).astype(jnp.bfloat16)))
    _, (kgrads, vgrads) = lax.scan(backward, zero_state, order, reverse=True)
    return (query_grad, kgrads.reshape(TOKENS, width), vgrads.reshape(TOKENS, width))
```

```python
import jax
import jax.numpy as jnp
from jax import lax
from jax.experimental import pallas as pl
from jax.experimental.pallas import tpu as pltpu
from jax.sharding import PartitionSpec as P

HEAD_DIM = 128
GROUP = 512
NZ = 12
NX, NY, NC = 4, 8, 2
NM = NX * NC
ARC = 4
ROWS = HEAD_DIM // ARC
MESH = pl.DeviceIdType.MESH
F32 = jnp.float32
BF16 = jnp.bfloat16
FAR_FIRST = (6, 5, 7, 4, 8, 3, 9, 2, 10, 1, 11)
NEAR = (2, 1, -1)


def dot(a, b):
    return lax.dot_general(a, b, (((1,), (0,)), ((), ())), preferred_element_type=F32)


def dot_nt(a, b):
    return lax.dot_general(a, b, (((1,), (1,)), ((), ())), preferred_element_type=F32)


def split(x):
    hi = x.astype(BF16)
    return hi, (x - hi.astype(F32)).astype(BF16)


class Scan:
    def __init__(self, z, head, earlier, refs):
        self.z, self.head, self.earlier = z, head, earlier
        self.src, self.near, self.out, self.inb, self.s1, self.r1, self.s2, self.r2 = refs

    def before(self, i, j):
        return i < j if self.earlier else i > j

    def first(self):
        copies = []
        for n, off in enumerate(NEAR):
            to = (self.z + off + NZ) % NZ
            copies.append(pltpu.make_async_remote_copy(
                src_ref=self.src.at[to % ARC], dst_ref=self.near.at[n],
                send_sem=self.s1.at[n], recv_sem=self.r1.at[n],
                device_id=(to, self.head), device_id_type=MESH))
        return copies

    def second(self):
        copies = []
        for t in FAR_FIRST:
            to = (self.z + t) % NZ
            copies.append(pltpu.make_async_remote_copy(
                src_ref=self.out.at[t], dst_ref=self.inb.at[t],
                send_sem=self.s2.at[t], recv_sem=self.r2.at[t],
                device_id=(to, self.head), device_id_type=MESH))
        return copies

    def start(self):
        self.c1 = self.first()
        for copy in self.c1:
            copy.start()

    def forward(self):
        for copy in self.c1:
            copy.wait()
        mine = [(self.z, self.src[self.z % ARC])]
        for n, off in enumerate(NEAR):
            mine.append(((self.z - off + NZ) % NZ, self.near[n]))
        self.c2 = self.second()
        for n, t in enumerate((*FAR_FIRST, 0)):
            to = (self.z + t) % NZ
            total = jnp.zeros((ROWS, HEAD_DIM), F32)
            for i, piece in mine:
                total = total + jnp.where(self.before(i, to), piece, 0.0)
            self.out[t] = total
            if t:
                self.c2[n].start()

    def finish(self, result):
        for copy in self.c2:
            copy.wait()
        for r in range(ARC):
            first = self.out[0] if r == 0 else self.inb[r]
            result[(self.z - r + NZ) % ARC] = first + self.inb[r + 4] + (self.inb[r + 8])


def kernel(blocks, width, q_hbm, k_hbm, v_hbm, gain_ref, og_hbm, qg_hbm, kg_hbm, vg_hbm,
           q, k, v, og, qg, kg, vg, vt, kt, ut, at, sct, agt, ag, kgf, vgf,
           kvt, sth, stl, st, stdh, stdl, adj, ext,
           src1, near1, out1, in1, src2, near2, out2, in2,
           stat, mstat, xin, yin,
           lsem, osem, s11, r11, s12, r12, s21, r21, s22, r22, sx, rx, sy, ry):
    z = lax.axis_index("ctx")
    head = lax.axis_index("head")
    core = head % NC
    y = (head // NC) % NY
    x = head // (NC * NY)
    m = x * NC + core

    loads = [pltpu.make_async_copy(a, b, lsem.at[n])
             for n, (a, b) in enumerate(((k_hbm, k), (v_hbm, v), (q_hbm, q), (og_hbm, og)))]
    for copy in loads:
        copy.start()

    barrier = pltpu.get_barrier_semaphore()
    xpeers, ypeers = [], []
    for d in range(1, NM):
        to = (m + d) % NM
        xpeers.append(((to // NC) * NY + y) * NC + to % NC)
    for d in range(1, NY):
        ypeers.append((x * NY + (y + d) % NY) * NC + core)
    for t in FAR_FIRST:
        pl.semaphore_signal(barrier, inc=1, device_id=((z + t) % NZ, head), device_id_type=MESH)
    for to in ypeers + xpeers:
        pl.semaphore_signal(barrier, inc=1, device_id=(z, to), device_id_type=MESH)

    loads[0].wait()
    loads[1].wait()
    total = jnp.zeros((HEAD_DIM, HEAD_DIM), F32)
    for n in range(blocks):
        vt[n] = v[n].T
        kvt[n] = total
        total = total + dot(vt[n], k[n])
    src1[...] = total.reshape(ARC, ROWS, HEAD_DIM)

    pl.semaphore_wait(barrier, NZ - 1 + NM - 1 + NY - 1)
    scan1 = Scan(z, head, True, (src1, near1, out1, in1, s11, r11, s12, r12))
    scan1.start()

    row = lax.broadcasted_iota(jnp.int32, (GROUP, GROUP), 0)
    col = lax.broadcasted_iota(jnp.int32, (GROUP, GROUP), 1)
    keep = row <= col
    gain = gain_ref[...]

    def local_scores(n):
        sct[n] = jnp.where(keep, dot_nt(k[n], q[n]), 0.0).astype(BF16)
        at[n] = dot(vt[n], sct[n])

    def local_rest(n):
        ut[n] = (og[n].astype(F32) * gain).T
        kt[n] = k[n].T

    loads[2].wait()
    loads[3].wait()
    for n in range(blocks // 2):
        local_scores(n)
    scan1.forward()
    for n in range(blocks // 2, blocks):
        local_scores(n)
    for n in range(blocks):
        local_rest(n)
    scan1.finish(ext)

    tiles = GROUP // HEAD_DIM
    earlier = ext[...].reshape(HEAD_DIM, HEAD_DIM)
    xcopies, ycopies = [], {}
    for n in range(blocks):
        state = earlier + kvt[n]
        st[n] = state
        hi, lo = split(state)
        a = at[n] + dot_nt(hi, q[n]) + dot_nt(lo, q[n])
        at[n] = a
        power = jnp.sum(a * a, axis=0, keepdims=True)
        cross = jnp.sum(a * ut[n], axis=0, keepdims=True)
        for c in range(tiles):
            stat[n, c : c + 1, :] = power[:, c * HEAD_DIM : (c + 1) * HEAD_DIM]
            stat[n, tiles + c : tiles + c + 1, :] = cross[:, c * HEAD_DIM : (c + 1) * HEAD_DIM]
        for d in range(1, NM):
            copy = pltpu.make_async_remote_copy(
                src_ref=stat.at[n], dst_ref=xin.at[n, d - 1],
                send_sem=sx.at[n, d - 1], recv_sem=rx.at[n, d - 1],
                device_id=(z, xpeers[d - 1]), device_id_type=MESH)
            copy.start()
            xcopies.append(copy)
    for n in range(blocks):
        total = stat[n]
        for d in range(1, NM):
            xcopies[n * (NM - 1) + d - 1].wait()
            total = total + xin[n, d - 1]
        mstat[n] = total
        for d in sorted(range(1, NY), key=lambda d: -min(d, NY - d)):
            copy = pltpu.make_async_remote_copy(
                src_ref=mstat.at[n], dst_ref=yin.at[n, d - 1],
                send_sem=sy.at[n, d - 1], recv_sem=ry.at[n, d - 1],
                device_id=(z, ypeers[d - 1]), device_id_type=MESH)
            copy.start()
            ycopies[n, d] = copy
    for n in range(blocks):
        stdh[n], stdl[n] = split(st[n].T)
    suffix = jnp.zeros((HEAD_DIM, HEAD_DIM), F32)
    for n in range(blocks):
        total = mstat[n]
        for d in range(1, NY):
            ycopies[n, d].wait()
            total = total + yin[n, d - 1]
        ratio = lax.rsqrt(total[:tiles] / width + 1e-06)
        scale = ratio * ratio * ratio * (total[tiles:] / width)
        for c in range(tiles):
            part = slice(c * HEAD_DIM, (c + 1) * HEAD_DIM)
            agt[n, :, part] = (ratio[c : c + 1] * ut[n, :, part] - at[n, :, part] * scale[c : c + 1]).astype(BF16)
        adj[n] = dot(agt[n], q[n])
    for n in reversed(range(blocks)):
        own = adj[n]
        adj[n] = suffix
        suffix = suffix + own
    src2[...] = suffix.reshape(ARC, ROWS, HEAD_DIM)
    scan2 = Scan(z, head, False, (src2, near2, out2, in2, s21, r21, s22, r22))
    scan2.start()

    def local_grads(n):
        bft = jnp.where(keep, dot(v[n], agt[n]), 0.0).astype(BF16)
        qgt = dot(kt[n], bft) + dot(stdh[n], agt[n]) + dot(stdl[n], agt[n])
        qg[n] = qgt.T.astype(BF16)
        kgf[n] = dot(bft, q[n])
        ag[n] = agt[n].T
        vgf[n] = dot(sct[n], ag[n])

    for n in range(blocks // 2):
        local_grads(n)
    scan2.forward()
    for n in range(blocks // 2, blocks):
        local_grads(n)
    out_q = pltpu.make_async_copy(qg, qg_hbm, osem.at[0])
    out_q.start()
    scan2.finish(ext)
    later = ext[...].reshape(HEAD_DIM, HEAD_DIM)
    for n in range(blocks):
        hi, lo = split(later + adj[n])
        kg[n] = (kgf[n] + dot(v[n], hi) + dot(v[n], lo)).astype(BF16)
        vg[n] = (vgf[n] + dot_nt(k[n], hi) + dot_nt(k[n], lo)).astype(BF16)
    out_k = pltpu.make_async_copy(kg, kg_hbm, osem.at[1])
    out_v = pltpu.make_async_copy(vg, vg_hbm, osem.at[2])
    out_k.start()
    out_v.start()
    out_q.wait()
    out_k.wait()
    out_v.wait()


def per_device(queries, keys, values, norm_gain, out_grad):
    tokens = queries.shape[0]
    blocks = tokens // GROUP
    width = lax.axis_size("head") * HEAD_DIM
    nat = (blocks, GROUP, HEAD_DIM)
    tra = (blocks, HEAD_DIM, GROUP)
    sq = (blocks, HEAD_DIM, HEAD_DIM)
    V = pltpu.VMEM
    D = pltpu.SemaphoreType.DMA
    piece = (ROWS, HEAD_DIM)
    srows = 2 * GROUP // HEAD_DIM
    zbuf = [V((ARC, *piece), F32), V((len(NEAR), *piece), F32), V((NZ, *piece), F32), V((NZ, *piece), F32)]
    zsem = [D((len(NEAR),)), D((len(NEAR),)), D((NZ,)), D((NZ,))]
    anyspec = pl.BlockSpec(memory_space=pl.ANY)
    out = pl.pallas_call(
        lambda *refs: kernel(blocks, width, *refs),
        out_shape=[jax.ShapeDtypeStruct(nat, BF16)] * 3,
        in_specs=[anyspec] * 3 + [pl.BlockSpec(memory_space=pltpu.VMEM)] + [anyspec],
        out_specs=[anyspec] * 3,
        scratch_shapes=[V(nat, BF16)] * 7
        + [V(tra, BF16), V(tra, BF16), V(tra, F32), V(tra, F32), V((blocks, GROUP, GROUP), BF16),
           V(tra, BF16), V(nat, BF16), V(nat, F32), V(nat, F32),
           V(sq, F32), V(sq, BF16), V(sq, BF16), V(sq, F32), V(sq, BF16), V(sq, BF16), V(sq, F32),
           V((ARC, *piece), F32)]
        + zbuf + zbuf
        + [V((blocks, srows, HEAD_DIM), F32), V((blocks, srows, HEAD_DIM), F32),
           V((blocks, NM - 1, srows, HEAD_DIM), F32), V((blocks, NY - 1, srows, HEAD_DIM), F32)]
        + [D((4,)), D((3,))] + zsem + zsem
        + [D((blocks, NM - 1))] * 2 + [D((blocks, NY - 1))] * 2,
        compiler_params=pltpu.CompilerParams(collective_id=0, has_side_effects=True),
        name="attention_backward",
    )(queries.reshape(nat), keys.reshape(nat), values.reshape(nat),
      norm_gain.reshape(1, HEAD_DIM), out_grad.reshape(nat))
    return tuple(o.reshape(tokens, HEAD_DIM) for o in out)


def solution(mesh):
    return jax.shard_map(
        per_device,
        mesh=mesh,
        in_specs=(
            P("ctx", "head"),
            P("ctx", "head"),
            P("ctx", "head"),
            P("head"),
            P("ctx", "head"),
        ),
        out_specs=(P("ctx", "head"), P("ctx", "head"), P("ctx", "head")),
        check_vma=False,
    )
```

```python
import jax
import jax.numpy as jnp
from jax import lax
from jax.experimental import pallas as pl
from jax.experimental.pallas import tpu as pltpu
from jax.sharding import PartitionSpec as P

HEAD_DIM = 128
GROUP = 512
NZ = 12
NX, NY, NC = 4, 8, 2
NM = NX * NC
ARC = 4
ROWS = HEAD_DIM // ARC
MESH = pl.DeviceIdType.MESH
KEPT = pltpu.VMEM
VMEM_LIMIT = 40 * 1024 * 1024
F32 = jnp.float32
BF16 = jnp.bfloat16
FAR_FIRST = (6, 5, 7, 4, 8, 3, 9, 2, 10, 1, 11)
NEAR = (2, 1, -1)


def dot(a, b):
    return lax.dot_general(a, b, (((1,), (0,)), ((), ())), preferred_element_type=F32)


def dot_nt(a, b):
    return lax.dot_general(a, b, (((1,), (1,)), ((), ())), preferred_element_type=F32)


def split(x):
    hi = x.astype(BF16)
    return hi, (x - hi.astype(F32)).astype(BF16)


class Scan:
    def __init__(self, z, head, earlier, refs):
        self.z, self.head, self.earlier = z, head, earlier
        self.src, self.near, self.out, self.inb, self.s1, self.r1, self.s2, self.r2 = refs

    def before(self, i, j):
        return i < j if self.earlier else i > j

    def needed(self, owner, to):
        found = self.before(owner, to)
        for off in NEAR:
            found = jnp.logical_or(found, self.before((owner - off + NZ) % NZ, to))
        return found

    def from_(self, t):
        return self.needed((self.z - t + NZ) % NZ, self.z)

    def first(self):
        copies = []
        for n, off in enumerate(NEAR):
            to = (self.z + off + NZ) % NZ
            copies.append(pltpu.make_async_remote_copy(
                src_ref=self.src.at[to % ARC], dst_ref=self.near.at[n],
                send_sem=self.s1.at[n], recv_sem=self.r1.at[n],
                device_id=(to, self.head), device_id_type=MESH))
        return copies

    def second(self):
        copies = []
        for t in FAR_FIRST:
            to = (self.z + t) % NZ
            copies.append(pltpu.make_async_remote_copy(
                src_ref=self.out.at[t], dst_ref=self.inb.at[t],
                send_sem=self.s2.at[t], recv_sem=self.r2.at[t],
                device_id=(to, self.head), device_id_type=MESH))
        return copies

    def start(self):
        self.c1 = self.first()
        for copy in self.c1:
            copy.start()

    def forward(self):
        for copy in self.c1:
            copy.wait()
        mine = [(self.z, self.src[self.z % ARC])]
        for n, off in enumerate(NEAR):
            mine.append(((self.z - off + NZ) % NZ, self.near[n]))
        self.c2 = self.second()
        for n, t in enumerate((*FAR_FIRST, 0)):
            to = (self.z + t) % NZ
            total = jnp.zeros((ROWS, HEAD_DIM), F32)
            for i, piece in mine:
                total = total + jnp.where(self.before(i, to), piece, 0.0)
            self.out[t] = total
            if t:
                pl.when(self.needed(self.z, to))(self.c2[n].start)

    def finish(self, result):
        for t, copy in zip(FAR_FIRST, self.c2):
            pl.when(self.needed(self.z, (self.z + t) % NZ))(copy.wait_send)
            pl.when(self.from_(t))(copy.wait_recv)
        for r in range(ARC):
            total = jnp.zeros((ROWS, HEAD_DIM), F32)
            for t in range(r, NZ, ARC):
                total = total + (jnp.where(self.from_(t), self.inb[t], 0.0) if t else self.out[0])
            result[(self.z - r + NZ) % ARC] = total


def kernel(blocks, width, q_hbm, k_hbm, v_hbm, gain_hbm, og_hbm,
           qg, kgf, vgf, k, v, adjh, adjl,
           q, og, gain_ref, vt, kt, ut, at, sct, agt, ag, kvt, st, stdh, stdl, adj, ext,
           src1, near1, out1, in1, src2, near2, out2, in2,
           stat, mstat, xin, yin,
           lsem, greet, s11, r11, s12, r12, s21, r21, s22, r22, sx, rx, sy, ry):
    z = lax.axis_index("ctx")
    head = lax.axis_index("head")
    core = head % NC
    y = (head // NC) % NY
    x = head // (NC * NY)
    m = x * NC + core

    loads = [pltpu.make_async_copy(a, b, lsem.at[n])
             for n, (a, b) in enumerate(((k_hbm, k), (v_hbm, v), (q_hbm, q), (og_hbm, og), (gain_hbm, gain_ref)))]
    for copy in loads:
        copy.start()

    barrier = pltpu.get_barrier_semaphore()
    xpeers, ypeers = [], []
    for d in range(1, NM):
        to = (m + d) % NM
        xpeers.append(((to // NC) * NY + y) * NC + to % NC)
    for d in range(1, NY):
        ypeers.append((x * NY + (y + d) % NY) * NC + core)
    znear = [(z + d + NZ) % NZ for d in (1, -1, 2, -2)]
    ynear = [ypeers[d - 1] for d in sorted({d % NY for d in (1, -1, 2, -2)} - {0})]
    for to in znear:
        pl.semaphore_signal(barrier, inc=1, device_id=(to, head), device_id_type=MESH)
    for to in xpeers + ynear:
        pl.semaphore_signal(barrier, inc=1, device_id=(z, to), device_id_type=MESH)

    def pass_on_z(n):
        for to in znear[2:]:
            pl.semaphore_signal(greet.at[n], inc=1, device_id=(to, head), device_id_type=MESH)

    loads[0].wait()
    loads[1].wait()
    total = jnp.zeros((HEAD_DIM, HEAD_DIM), F32)
    for n in range(blocks):
        vt[n] = v[n].T
        kvt[n] = total
        total = total + dot(vt[n], k[n])
    src1[...] = total.reshape(ARC, ROWS, HEAD_DIM)

    pl.semaphore_wait(barrier, len(znear) + len(xpeers) + len(ynear))
    scan1 = Scan(z, head, True, (src1, near1, out1, in1, s11, r11, s12, r12))
    scan1.start()
    pass_on_z(0)
    if NY > 5:
        for d in (2, NY - 2):
            pl.semaphore_signal(greet.at[2], inc=1, device_id=(z, ypeers[d - 1]), device_id_type=MESH)

    row = lax.broadcasted_iota(jnp.int32, (GROUP, GROUP), 0)
    col = lax.broadcasted_iota(jnp.int32, (GROUP, GROUP), 1)
    keep = row <= col
    loads[4].wait()
    gain = gain_ref[...]

    def local_scores(n):
        sct[n] = jnp.where(keep, dot_nt(k[n], q[n]), 0.0).astype(BF16)
        at[n] = dot(vt[n], sct[n])

    def local_rest(n):
        ut[n] = (og[n].astype(F32) * gain).T
        kt[n] = k[n].T

    loads[2].wait()
    loads[3].wait()
    for n in range(blocks // 2):
        local_scores(n)
    pl.semaphore_wait(greet.at[0], 2)
    pass_on_z(1)
    for n in range(blocks // 2, blocks - 1):
        local_scores(n)
    pl.semaphore_wait(greet.at[1], 2)
    scan1.forward()
    local_scores(blocks - 1)
    for n in range(blocks):
        local_rest(n)
    scan1.finish(ext)

    tiles = GROUP // HEAD_DIM
    earlier = ext[...].reshape(HEAD_DIM, HEAD_DIM)
    xcopies, ycopies = [], {}
    for n in range(blocks):
        state = earlier + kvt[n]
        st[n] = state
        hi, lo = split(state)
        a = at[n] + dot_nt(hi, q[n]) + dot_nt(lo, q[n])
        at[n] = a
        power = jnp.sum(a * a, axis=0, keepdims=True)
        cross = jnp.sum(a * ut[n], axis=0, keepdims=True)
        for c in range(tiles):
            stat[n, c : c + 1, :] = power[:, c * HEAD_DIM : (c + 1) * HEAD_DIM]
            stat[n, tiles + c : tiles + c + 1, :] = cross[:, c * HEAD_DIM : (c + 1) * HEAD_DIM]
        for d in range(1, NM):
            copy = pltpu.make_async_remote_copy(
                src_ref=stat.at[n], dst_ref=xin.at[n, d - 1],
                send_sem=sx.at[n, d - 1], recv_sem=rx.at[n, d - 1],
                device_id=(z, xpeers[d - 1]), device_id_type=MESH)
            copy.start()
            xcopies.append(copy)
    if NY > 5:
        pl.semaphore_wait(greet.at[2], 2)
    for n in range(blocks):
        total = stat[n]
        for d in range(1, NM):
            xcopies[n * (NM - 1) + d - 1].wait()
            total = total + xin[n, d - 1]
        mstat[n] = total
        for d in sorted(range(1, NY), key=lambda d: -min(d, NY - d)):
            copy = pltpu.make_async_remote_copy(
                src_ref=mstat.at[n], dst_ref=yin.at[n, d - 1],
                send_sem=sy.at[n, d - 1], recv_sem=ry.at[n, d - 1],
                device_id=(z, ypeers[d - 1]), device_id_type=MESH)
            copy.start()
            ycopies[n, d] = copy
    for n in range(blocks):
        stdh[n], stdl[n] = split(st[n].T)
    suffix = jnp.zeros((HEAD_DIM, HEAD_DIM), F32)
    for n in range(blocks):
        total = mstat[n]
        for d in range(1, NY):
            ycopies[n, d].wait()
            total = total + yin[n, d - 1]
        ratio = lax.rsqrt(total[:tiles] / width + 1e-06)
        scale = ratio * ratio * ratio * (total[tiles:] / width)
        for c in range(tiles):
            part = slice(c * HEAD_DIM, (c + 1) * HEAD_DIM)
            agt[n, :, part] = (ratio[c : c + 1] * ut[n, :, part] - at[n, :, part] * scale[c : c + 1]).astype(BF16)
        adj[n] = dot(agt[n], q[n])
    for n in reversed(range(blocks)):
        own = adj[n]
        adj[n] = suffix
        suffix = suffix + own
    src2[...] = suffix.reshape(ARC, ROWS, HEAD_DIM)
    scan2 = Scan(z, head, False, (src2, near2, out2, in2, s21, r21, s22, r22))
    scan2.start()

    def local_grads(n):
        bft = jnp.where(keep, dot(v[n], agt[n]), 0.0).astype(BF16)
        qgt = dot(kt[n], bft) + dot(stdh[n], agt[n]) + dot(stdl[n], agt[n])
        qg[n] = qgt.T.astype(BF16)
        kgf[n] = dot(bft, q[n])
        ag[n] = agt[n].T
        vgf[n] = dot(sct[n], ag[n])

    for n in range(blocks // 2):
        local_grads(n)
    scan2.forward()
    for n in range(blocks // 2, blocks):
        local_grads(n)
    scan2.finish(ext)
    later = ext[...].reshape(HEAD_DIM, HEAD_DIM)
    for n in range(blocks):
        adjh[n], adjl[n] = split(later + adj[n])


def finish(blocks, qg, kgf, vgf, k, v, adjh, adjl, qg_hbm, kg_hbm, vg_hbm, kg, vg, sem):
    copies = [pltpu.make_async_copy(qg, qg_hbm, sem.at[0, blocks])]
    copies[0].start()
    for n in range(blocks):
        hi, lo = adjh[n], adjl[n]
        kg[n] = (kgf[n] + dot(v[n], hi) + dot(v[n], lo)).astype(BF16)
        copies.append(pltpu.make_async_copy(kg.at[n], kg_hbm.at[n], sem.at[0, n]))
        copies[-1].start()
        vg[n] = (vgf[n] + dot_nt(k[n], hi) + dot_nt(k[n], lo)).astype(BF16)
        copies.append(pltpu.make_async_copy(vg.at[n], vg_hbm.at[n], sem.at[1, n]))
        copies[-1].start()
    for copy in copies:
        copy.wait()


def per_device(queries, keys, values, norm_gain, out_grad):
    tokens = queries.shape[0]
    blocks = tokens // GROUP
    width = lax.axis_size("head") * HEAD_DIM
    nat = (blocks, GROUP, HEAD_DIM)
    tra = (blocks, HEAD_DIM, GROUP)
    sq = (blocks, HEAD_DIM, HEAD_DIM)
    V = pltpu.VMEM
    D = pltpu.SemaphoreType.DMA
    piece = (ROWS, HEAD_DIM)
    srows = 2 * GROUP // HEAD_DIM
    zbuf = [V((ARC, *piece), F32), V((len(NEAR), *piece), F32), V((NZ, *piece), F32), V((NZ, *piece), F32)]
    zsem = [D((len(NEAR),)), D((len(NEAR),)), D((NZ,)), D((NZ,))]
    anyspec = pl.BlockSpec(memory_space=pl.ANY)
    hbmspec = pl.BlockSpec(memory_space=pltpu.HBM)
    vspec = pl.BlockSpec(memory_space=pltpu.VMEM)
    out = pl.pallas_call(
        lambda *refs: kernel(blocks, width, *refs),
        out_shape=[KEPT(nat, BF16), KEPT(nat, F32), KEPT(nat, F32), KEPT(nat, BF16), KEPT(nat, BF16),
                   KEPT(sq, BF16), KEPT(sq, BF16)],
        in_specs=[hbmspec] * 5,
        out_specs=[vspec] * 7,
        scratch_shapes=[V(nat, BF16)] * 2
        + [V((1, HEAD_DIM), F32), V(tra, BF16), V(tra, BF16), V(tra, F32), V(tra, F32), V((blocks, GROUP, GROUP), BF16),
           V(tra, BF16), V(nat, BF16),
           V(sq, F32), V(sq, F32), V(sq, BF16), V(sq, BF16), V(sq, F32),
           V((ARC, *piece), F32)]
        + zbuf + zbuf
        + [V((blocks, srows, HEAD_DIM), F32), V((blocks, srows, HEAD_DIM), F32),
           V((blocks, NM - 1, srows, HEAD_DIM), F32), V((blocks, NY - 1, srows, HEAD_DIM), F32)]
        + [D((5,)), pltpu.SemaphoreType.REGULAR((3,))] + zsem + zsem
        + [D((blocks, NM - 1))] * 2 + [D((blocks, NY - 1))] * 2,
        compiler_params=pltpu.CompilerParams(collective_id=0, has_side_effects=True, vmem_limit_bytes=VMEM_LIMIT),
        name="attention_backward",
    )(*(pltpu.with_memory_space_constraint(a.reshape(nat), pltpu.HBM) for a in (queries, keys, values)),
      pltpu.with_memory_space_constraint(norm_gain.reshape(1, HEAD_DIM), pltpu.HBM),
      pltpu.with_memory_space_constraint(out_grad.reshape(nat), pltpu.HBM))
    out = pl.pallas_call(
        lambda *refs: finish(blocks, *refs),
        out_shape=[jax.ShapeDtypeStruct(nat, BF16)] * 3,
        in_specs=[vspec] * 7,
        out_specs=[anyspec] * 3,
        scratch_shapes=[V(nat, BF16)] * 2 + [D((2, blocks + 1))],
        compiler_params=pltpu.CompilerParams(vmem_limit_bytes=VMEM_LIMIT // 4),
        name="finish",
    )(*(pltpu.with_memory_space_constraint(o, pltpu.VMEM) for o in out))
    return tuple(o.reshape(tokens, HEAD_DIM) for o in out)


def solution(mesh):
    return jax.shard_map(
        per_device,
        mesh=mesh,
        in_specs=(
            P("ctx", "head"),
            P("ctx", "head"),
            P("ctx", "head"),
            P("head"),
            P("ctx", "head"),
        ),
        out_specs=(P("ctx", "head"), P("ctx", "head"), P("ctx", "head")),
        check_vma=False,
    )
```

```python
import jax
import jax.numpy as jnp
from jax import lax
from jax.experimental import pallas as pl
from jax.experimental.pallas import tpu as pltpu
from jax.sharding import PartitionSpec as P

HEAD_DIM = 128
GROUP = 512
NZ = 12
NX, NY, NC = 4, 8, 2
NM = NX * NC
ARC = 4
ROWS = HEAD_DIM // ARC
MESH = pl.DeviceIdType.MESH
KEPT = pltpu.VMEM
VMEM_LIMIT = 40 * 1024 * 1024
F32 = jnp.float32
BF16 = jnp.bfloat16


def dot(a, b):
    return lax.dot_general(a, b, (((1,), (0,)), ((), ())), preferred_element_type=F32)


def dot_nt(a, b):
    return lax.dot_general(a, b, (((1,), (1,)), ((), ())), preferred_element_type=F32)


def split(x):
    hi = x.astype(BF16)
    return hi, (x - hi.astype(F32)).astype(BF16)


class Scan:
    def __init__(self, z, head, step, refs):
        self.z, self.head, self.step, self.c2 = z, head, step, {}
        self.group, self.place = z // ARC, z % ARC
        self.end = NZ - 1 if step > 0 else 0
        self.src, self.near, self.out, self.inb, self.s1, self.r1, self.s2, self.r2 = refs

    def mate(self, off):
        return self.group * ARC + (self.place + off + ARC) % ARC

    def copy(self, src, dst, send, recv, to):
        return pltpu.make_async_remote_copy(
            src_ref=src, dst_ref=dst, send_sem=send, recv_sem=recv, device_id=(to, self.head), device_id_type=MESH)

    def start(self):
        self.c1 = [self.copy(self.src.at[(self.place + off) % ARC], self.near.at[off - 1],
                             self.s1.at[off - 1], self.r1.at[off - 1], self.mate(off)) for off in range(1, ARC)]
        for copy in self.c1:
            pl.when(self.z != self.end)(copy.start)

    def gather(self):
        for off, copy in enumerate(self.c1, 1):
            pl.when(self.z != self.end)(copy.wait_send)
            pl.when(self.mate(-off) != self.end)(copy.wait_recv)
        return [(self.z, self.src[self.place])] + [(self.mate(-off), self.near[off - 1]) for off in range(1, ARC)]

    def before(self, i, to):
        return i < to if self.step > 0 else i > to

    def there(self, k):
        to = self.group + self.step * k
        return jnp.logical_and(to >= 0, to < NZ // ARC)

    def pass_on(self, greet):
        self.mine = self.gather()
        total = jnp.zeros((ROWS, HEAD_DIM), F32)
        for _, piece in self.mine:
            total = total + piece
        self.out[ARC] = total
        self.on = {}
        for k in range(1, NZ // ARC):
            to = (self.z + self.step * ARC * k + NZ) % NZ
            self.on[k] = self.copy(self.out.at[ARC], self.inb.at[ARC + k], self.s2.at[ARC + k], self.r2.at[ARC + k], to)

            @pl.when(self.there(k))
            def _():
                pl.semaphore_wait(greet.at[k], 1)
                self.on[k].start()

    def share(self):
        before = jnp.zeros((ROWS, HEAD_DIM), F32)
        for k in range(1, NZ // ARC):
            pl.when(self.there(-k))(self.on[k].wait_recv)
            before = before + jnp.where(self.there(-k), self.inb[ARC + k], 0.0)
        self.c2 = []
        for off in range(ARC):
            total = before
            for i, piece in self.mine:
                total = total + jnp.where(self.before(i, self.mate(off)), piece, 0.0)
            self.out[off] = total
            if off:
                self.c2.append(self.copy(self.out.at[off], self.inb.at[off],
                                         self.s2.at[off], self.r2.at[off], self.mate(off)))
                self.c2[-1].start()

    def finish(self, result):
        result[self.place] = self.out[0]
        for off, copy in enumerate(self.c2, 1):
            copy.wait()
            result[(self.place - off + ARC) % ARC] = self.inb[off]

    def close(self):
        for k, copy in self.on.items():
            pl.when(self.there(k))(copy.wait_send)


class AdjointScan(Scan):
    def targets(self, k):
        for place in range(ARC):
            to = ((self.group + self.step * k + NZ) % (NZ // ARC)) * ARC + place
            sends = self.place != place if k == 0 else self.there(k)
            yield k * ARC + place, to, sends

    def spread(self, k, mine):
        for n, to, sends in self.targets(k):
            total = jnp.zeros((ROWS, HEAD_DIM), F32)
            for i, piece in mine:
                total = total + (jnp.where(self.before(i, to), piece, 0.0) if k == 0 else piece)
            self.out[n] = total
            self.c2[n] = self.copy(self.out.at[n], self.inb.at[self.z], self.s2.at[n], self.r2.at[self.z], to)
            pl.when(sends)(self.c2[n].start)

    def crosses(self, owner, to):
        between = to // ARC - owner // ARC
        return jnp.logical_and(owner != to, (between if self.step > 0 else -between) >= 0)

    def finish(self, result):
        for o in range(NZ):
            arrival = self.copy(self.out.at[0], self.inb.at[o], self.s2.at[0], self.r2.at[o], jnp.int32(o))
            pl.when(self.crosses(o, self.z))(arrival.wait_recv)
        for r in range(ARC):
            total = jnp.where(self.place == r, self.out[self.place], 0.0)
            for o in range(r, NZ, ARC):
                total = total + jnp.where(self.crosses(o, self.z), self.inb[o], 0.0)
            result[r] = total

    def close(self):
        for k in range(NZ // ARC):
            for n, _, sends in self.targets(k):
                pl.when(sends)(self.c2[n].wait_send)


def kernel(blocks, width, q_hbm, k_hbm, v_hbm, gain_hbm, og_hbm,
           qg, kgf, vgf, k, v, adjh, adjl,
           q, og, gain_ref, vt, kt, ut, at, sct, agt, ag, kvt, st, stdh, stdl, adj, ext,
           src1, near1, out1, in1, src2, near2, out2, in2,
           stat, mstat, xin, yin,
           lsem, greet, s11, r11, s12, r12, s21, r21, s22, r22, sx, rx, sy, ry):
    z = lax.axis_index("ctx")
    head = lax.axis_index("head")
    core = head % NC
    y = (head // NC) % NY
    x = head // (NC * NY)
    m = x * NC + core

    loads = [pltpu.make_async_copy(a, b, lsem.at[n])
             for n, (a, b) in enumerate(((k_hbm, k), (v_hbm, v), (q_hbm, q), (og_hbm, og), (gain_hbm, gain_ref)))]
    for copy in loads:
        copy.start()

    barrier = pltpu.get_barrier_semaphore()
    xpeers, ypeers = [], []
    for d in range(1, NM):
        to = (m + d) % NM
        xpeers.append(((to // NC) * NY + y) * NC + to % NC)
    for d in range(1, NY):
        ypeers.append((x * NY + (y + d) % NY) * NC + core)
    scan1 = Scan(z, head, 1, (src1, near1, out1, in1, s11, r11, s12, r12))
    scan2 = AdjointScan(z, head, -1, (src2, near2, out2, in2, s21, r21, s22, r22))
    ynear = [ypeers[d - 1] for d in sorted({d % NY for d in (1, -1, 2, -2)} - {0})]
    for off in range(1, ARC):
        pl.semaphore_signal(barrier, inc=1, device_id=(scan1.mate(off), head), device_id_type=MESH)

    for g in range(1, NZ // ARC):
        @pl.when(scan1.there(g))
        def _():
            pl.semaphore_signal(barrier, inc=1, device_id=((z + ARC * g) % NZ, head), device_id_type=MESH)

    for to in xpeers + ynear:
        pl.semaphore_signal(barrier, inc=1, device_id=(z, to), device_id_type=MESH)

    def products():
        loads[0].wait()
        loads[1].wait()
        total = jnp.zeros((HEAD_DIM, HEAD_DIM), F32)
        for n in range(blocks):
            vt[n] = v[n].T
            kvt[n] = total
            total = total + dot(vt[n], k[n])
        src1[...] = total.reshape(ARC, ROWS, HEAD_DIM)

    pl.when(z < NZ - 1)(products)
    pl.semaphore_wait(barrier, z // ARC + (ARC - 1 + len(xpeers) + len(ynear)))
    for g in range(1, NZ // ARC):
        @pl.when(scan2.there(g))
        def _():
            pl.semaphore_signal(greet.at[g], inc=1, device_id=((z + NZ - ARC * g) % NZ, head), device_id_type=MESH)

    pl.when(z == NZ - 1)(products)
    scan1.start()
    if NY > 5:
        for d in (2, NY - 2):
            pl.semaphore_signal(greet.at[0], inc=1, device_id=(z, ypeers[d - 1]), device_id_type=MESH)

    row = lax.broadcasted_iota(jnp.int32, (GROUP, GROUP), 0)
    col = lax.broadcasted_iota(jnp.int32, (GROUP, GROUP), 1)
    keep = row <= col
    loads[4].wait()
    gain = gain_ref[...]

    def local_scores(n):
        sct[n] = jnp.where(keep, dot_nt(k[n], q[n]), 0.0).astype(BF16)
        at[n] = dot(vt[n], sct[n])

    def local_rest(n):
        ut[n] = (og[n].astype(F32) * gain).T
        kt[n] = k[n].T

    loads[2].wait()
    loads[3].wait()
    for n in range(blocks):
        local_scores(n)
    for n in range(blocks):
        local_rest(n)
    scan1.pass_on(greet)
    scan1.share()
    scan1.finish(ext)

    tiles = GROUP // HEAD_DIM
    earlier = ext[...].reshape(HEAD_DIM, HEAD_DIM)
    xcopies, ycopies = [], {}
    for n in range(blocks):
        state = earlier + kvt[n]
        st[n] = state
        hi, lo = split(state)
        a = at[n] + dot_nt(hi, q[n]) + dot_nt(lo, q[n])
        at[n] = a
        power = jnp.sum(a * a, axis=0, keepdims=True)
        cross = jnp.sum(a * ut[n], axis=0, keepdims=True)
        for c in range(tiles):
            stat[n, c : c + 1, :] = power[:, c * HEAD_DIM : (c + 1) * HEAD_DIM]
            stat[n, tiles + c : tiles + c + 1, :] = cross[:, c * HEAD_DIM : (c + 1) * HEAD_DIM]
        for d in range(1, NM):
            copy = pltpu.make_async_remote_copy(
                src_ref=stat.at[n], dst_ref=xin.at[n, d - 1],
                send_sem=sx.at[n, d - 1], recv_sem=rx.at[n, d - 1],
                device_id=(z, xpeers[d - 1]), device_id_type=MESH)
            copy.start()
            xcopies.append(copy)
    if NY > 5:
        pl.semaphore_wait(greet.at[0], 2)
    for n in range(blocks):
        total = stat[n]
        for d in range(1, NM):
            xcopies[n * (NM - 1) + d - 1].wait()
            total = total + xin[n, d - 1]
        mstat[n] = total
        for d in sorted(range(1, NY), key=lambda d: -min(d, NY - d)):
            copy = pltpu.make_async_remote_copy(
                src_ref=mstat.at[n], dst_ref=yin.at[n, d - 1],
                send_sem=sy.at[n, d - 1], recv_sem=ry.at[n, d - 1],
                device_id=(z, ypeers[d - 1]), device_id_type=MESH)
            copy.start()
            ycopies[n, d] = copy
    for n in range(blocks):
        stdh[n], stdl[n] = split(st[n].T)
    suffix = jnp.zeros((HEAD_DIM, HEAD_DIM), F32)
    for n in range(blocks):
        total = mstat[n]
        for d in range(1, NY):
            ycopies[n, d].wait()
            total = total + yin[n, d - 1]
        ratio = lax.rsqrt(total[:tiles] / width + 1e-06)
        scale = ratio * ratio * ratio * (total[tiles:] / width)
        for c in range(tiles):
            part = slice(c * HEAD_DIM, (c + 1) * HEAD_DIM)
            agt[n, :, part] = (ratio[c : c + 1] * ut[n, :, part] - at[n, :, part] * scale[c : c + 1]).astype(BF16)
        adj[n] = dot(agt[n], q[n])
    for n in reversed(range(blocks)):
        own = adj[n]
        adj[n] = suffix
        suffix = suffix + own
    src2[...] = suffix.reshape(ARC, ROWS, HEAD_DIM)
    scan2.start()

    def local_grads(n):
        bft = jnp.where(keep, dot(v[n], agt[n]), 0.0).astype(BF16)
        qgt = dot(kt[n], bft) + dot(stdh[n], agt[n]) + dot(stdl[n], agt[n])
        qg[n] = qgt.T.astype(BF16)
        kgf[n] = dot(bft, q[n])
        ag[n] = agt[n].T
        vgf[n] = dot(sct[n], ag[n])

    for n in range(blocks // 2):
        local_grads(n)
    mine = scan2.gather()
    for g in reversed(range(NZ // ARC)):
        scan2.spread(g, mine)
    for n in range(blocks // 2, blocks):
        local_grads(n)
    scan2.finish(ext)
    later = ext[...].reshape(HEAD_DIM, HEAD_DIM)
    for n in range(blocks):
        adjh[n], adjl[n] = split(later + adj[n])
    scan1.close()
    scan2.close()


def finish(blocks, qg, kgf, vgf, k, v, adjh, adjl, qg_hbm, kg_hbm, vg_hbm, kg, vg, sem):
    copies = [pltpu.make_async_copy(qg, qg_hbm, sem.at[0, blocks])]
    copies[0].start()
    for n in range(blocks):
        hi, lo = adjh[n], adjl[n]
        kg[n] = (kgf[n] + dot(v[n], hi) + dot(v[n], lo)).astype(BF16)
        copies.append(pltpu.make_async_copy(kg.at[n], kg_hbm.at[n], sem.at[0, n]))
        copies[-1].start()
        vg[n] = (vgf[n] + dot_nt(k[n], hi) + dot_nt(k[n], lo)).astype(BF16)
        copies.append(pltpu.make_async_copy(vg.at[n], vg_hbm.at[n], sem.at[1, n]))
        copies[-1].start()
    for copy in copies:
        copy.wait()


def per_device(queries, keys, values, norm_gain, out_grad):
    tokens = queries.shape[0]
    blocks = tokens // GROUP
    width = lax.axis_size("head") * HEAD_DIM
    nat = (blocks, GROUP, HEAD_DIM)
    tra = (blocks, HEAD_DIM, GROUP)
    sq = (blocks, HEAD_DIM, HEAD_DIM)
    V = pltpu.VMEM
    D = pltpu.SemaphoreType.DMA
    piece = (ROWS, HEAD_DIM)
    srows = 2 * GROUP // HEAD_DIM
    zbuf = [V((ARC, *piece), F32), V((ARC - 1, *piece), F32), V((NZ, *piece), F32), V((NZ, *piece), F32)]
    zsem = [D((ARC - 1,)), D((ARC - 1,)), D((NZ,)), D((NZ,))]
    anyspec = pl.BlockSpec(memory_space=pl.ANY)
    hbmspec = pl.BlockSpec(memory_space=pltpu.HBM)
    vspec = pl.BlockSpec(memory_space=pltpu.VMEM)
    out = pl.pallas_call(
        lambda *refs: kernel(blocks, width, *refs),
        out_shape=[KEPT(nat, BF16), KEPT(nat, F32), KEPT(nat, F32), KEPT(nat, BF16), KEPT(nat, BF16),
                   KEPT(sq, BF16), KEPT(sq, BF16)],
        in_specs=[hbmspec] * 5,
        out_specs=[vspec] * 7,
        scratch_shapes=[V(nat, BF16)] * 2
        + [V((1, HEAD_DIM), F32), V(tra, BF16), V(tra, BF16), V(tra, F32), V(tra, F32), V((blocks, GROUP, GROUP), BF16),
           V(tra, BF16), V(nat, BF16),
           V(sq, F32), V(sq, F32), V(sq, BF16), V(sq, BF16), V(sq, F32),
           V((ARC, *piece), F32)]
        + zbuf + zbuf
        + [V((blocks, srows, HEAD_DIM), F32), V((blocks, srows, HEAD_DIM), F32),
           V((blocks, NM - 1, srows, HEAD_DIM), F32), V((blocks, NY - 1, srows, HEAD_DIM), F32)]
        + [D((5,)), pltpu.SemaphoreType.REGULAR((NZ // ARC,))] + zsem + zsem
        + [D((blocks, NM - 1))] * 2 + [D((blocks, NY - 1))] * 2,
        compiler_params=pltpu.CompilerParams(collective_id=0, has_side_effects=True, vmem_limit_bytes=VMEM_LIMIT),
        name="attention_backward",
    )(*(pltpu.with_memory_space_constraint(a.reshape(nat), pltpu.HBM) for a in (queries, keys, values)),
      pltpu.with_memory_space_constraint(norm_gain.reshape(1, HEAD_DIM), pltpu.HBM),
      pltpu.with_memory_space_constraint(out_grad.reshape(nat), pltpu.HBM))
    out = pl.pallas_call(
        lambda *refs: finish(blocks, *refs),
        out_shape=[jax.ShapeDtypeStruct(nat, BF16)] * 3,
        in_specs=[vspec] * 7,
        out_specs=[anyspec] * 3,
        scratch_shapes=[V(nat, BF16)] * 2 + [D((2, blocks + 1))],
        compiler_params=pltpu.CompilerParams(vmem_limit_bytes=VMEM_LIMIT // 4),
        name="finish",
    )(*(pltpu.with_memory_space_constraint(o, pltpu.VMEM) for o in out))
    return tuple(o.reshape(tokens, HEAD_DIM) for o in out)


def solution(mesh):
    return jax.shard_map(
        per_device,
        mesh=mesh,
        in_specs=(
            P("ctx", "head"),
            P("ctx", "head"),
            P("ctx", "head"),
            P("head"),
            P("ctx", "head"),
        ),
        out_specs=(P("ctx", "head"), P("ctx", "head"), P("ctx", "head")),
        check_vma=False,
    )
```

```python
import jax
import jax.numpy as jnp
from jax import lax
from jax.experimental import pallas as pl
from jax.experimental.pallas import tpu as pltpu
from jax.sharding import PartitionSpec as P

HEAD_DIM = 128
GROUP = 512
NZ = 12
NX, NY, NC = 4, 8, 2
NM = NX * NC
ARC = 4
ROWS = HEAD_DIM // ARC
MESH = pl.DeviceIdType.MESH
KEPT = pltpu.VMEM
VMEM_LIMIT = 40 * 1024 * 1024
F32 = jnp.float32
BF16 = jnp.bfloat16


def dot(a, b):
    return lax.dot_general(a, b, (((1,), (0,)), ((), ())), preferred_element_type=F32)


def dot_nt(a, b):
    return lax.dot_general(a, b, (((1,), (1,)), ((), ())), preferred_element_type=F32)


def split(x):
    hi = x.astype(BF16)
    return hi, (x - hi.astype(F32)).astype(BF16)


class Scan:
    def __init__(self, z, head, step, refs):
        self.z, self.head, self.step, self.c2 = z, head, step, {}
        self.group, self.place = z // ARC, z % ARC
        self.end = NZ - 1 if step > 0 else 0
        self.src, self.near, self.out, self.inb, self.s1, self.r1, self.s2, self.r2 = refs

    def mate(self, off):
        return self.group * ARC + (self.place + off + ARC) % ARC

    def copy(self, src, dst, send, recv, to):
        return pltpu.make_async_remote_copy(
            src_ref=src, dst_ref=dst, send_sem=send, recv_sem=recv, device_id=(to, self.head), device_id_type=MESH)

    def start(self):
        self.c1 = [self.copy(self.src.at[(self.place + off) % ARC], self.near.at[off - 1],
                             self.s1.at[off - 1], self.r1.at[off - 1], self.mate(off)) for off in range(1, ARC)]
        for copy in self.c1:
            pl.when(self.z != self.end)(copy.start)

    def gather(self):
        for off, copy in enumerate(self.c1, 1):
            pl.when(self.z != self.end)(copy.wait_send)
            pl.when(self.mate(-off) != self.end)(copy.wait_recv)
        return [(self.z, self.src[self.place])] + [(self.mate(-off), self.near[off - 1]) for off in range(1, ARC)]

    def before(self, i, to):
        return i < to if self.step > 0 else i > to

    def there(self, k):
        to = self.group + self.step * k
        return jnp.logical_and(to >= 0, to < NZ // ARC)

    def pass_on(self, greet):
        self.mine = self.gather()
        total = jnp.zeros((ROWS, HEAD_DIM), F32)
        for _, piece in self.mine:
            total = total + piece
        self.out[ARC] = total
        self.on = {}
        for k in range(1, NZ // ARC):
            to = (self.z + self.step * ARC * k + NZ) % NZ
            self.on[k] = self.copy(self.out.at[ARC], self.inb.at[ARC + k], self.s2.at[ARC + k], self.r2.at[ARC + k], to)

            @pl.when(self.there(k))
            def _():
                pl.semaphore_wait(greet.at[k], 1)
                self.on[k].start()

    def share(self):
        before = jnp.zeros((ROWS, HEAD_DIM), F32)
        for k in range(1, NZ // ARC):
            pl.when(self.there(-k))(self.on[k].wait_recv)
            before = before + jnp.where(self.there(-k), self.inb[ARC + k], 0.0)
        self.c2 = []
        for off in range(ARC):
            total = before
            for i, piece in self.mine:
                total = total + jnp.where(self.before(i, self.mate(off)), piece, 0.0)
            self.out[off] = total
            if off:
                self.c2.append(self.copy(self.out.at[off], self.inb.at[off],
                                         self.s2.at[off], self.r2.at[off], self.mate(off)))
                self.c2[-1].start()

    def finish(self, result):
        result[self.place] = self.out[0]
        for off, copy in enumerate(self.c2, 1):
            copy.wait()
            result[(self.place - off + ARC) % ARC] = self.inb[off]

    def close(self):
        for k, copy in self.on.items():
            pl.when(self.there(k))(copy.wait_send)


class AdjointScan(Scan):
    def targets(self, k):
        for place in range(ARC):
            to = ((self.group + self.step * k + NZ) % (NZ // ARC)) * ARC + place
            sends = self.place != place if k == 0 else self.there(k)
            yield k * ARC + place, to, sends

    def spread(self, k, mine):
        for n, to, sends in self.targets(k):
            total = jnp.zeros((ROWS, HEAD_DIM), F32)
            for i, piece in mine:
                total = total + (jnp.where(self.before(i, to), piece, 0.0) if k == 0 else piece)
            self.out[n] = total
            self.c2[n] = self.copy(self.out.at[n], self.inb.at[self.z], self.s2.at[n], self.r2.at[self.z], to)
            pl.when(sends)(self.c2[n].start)

    def crosses(self, owner, to):
        between = to // ARC - owner // ARC
        return jnp.logical_and(owner != to, (between if self.step > 0 else -between) >= 0)

    def finish(self, result):
        for o in range(NZ):
            arrival = self.copy(self.out.at[0], self.inb.at[o], self.s2.at[0], self.r2.at[o], jnp.int32(o))
            pl.when(self.crosses(o, self.z))(arrival.wait_recv)
        for r in range(ARC):
            total = jnp.where(self.place == r, self.out[self.place], 0.0)
            for o in range(r, NZ, ARC):
                total = total + jnp.where(self.crosses(o, self.z), self.inb[o], 0.0)
            result[r] = total

    def close(self):
        for k in range(NZ // ARC):
            for n, _, sends in self.targets(k):
                pl.when(sends)(self.c2[n].wait_send)


def kernel(blocks, width, q_hbm, k_hbm, v_hbm, gain_hbm, og_hbm,
           qg, kgf, vgf, k, v, adjh, adjl,
           q, og, gain_ref, vt, kt, ut, at, sct, agt, ag, kvt, st, stdh, stdl, adj, ext,
           src1, near1, out1, in1, src2, near2, out2, in2,
           stat, mstat, xin, yin,
           lsem, greet, s11, r11, s12, r12, s21, r21, s22, r22, sx, rx, sy, ry):
    z = lax.axis_index("ctx")
    head = lax.axis_index("head")
    core = head % NC
    y = (head // NC) % NY
    x = head // (NC * NY)
    m = x * NC + core

    loads = [pltpu.make_async_copy(a, b, lsem.at[n])
             for n, (a, b) in enumerate(((k_hbm, k), (v_hbm, v), (q_hbm, q), (og_hbm, og), (gain_hbm, gain_ref)))]
    for copy in loads:
        copy.start()

    barrier = pltpu.get_barrier_semaphore()
    xpeers, ypeers = [], []
    for d in range(1, NM):
        to = (m + d) % NM
        xpeers.append(((to // NC) * NY + y) * NC + to % NC)
    for d in range(1, NY):
        ypeers.append((x * NY + (y + d) % NY) * NC + core)
    scan1 = Scan(z, head, 1, (src1, near1, out1, in1, s11, r11, s12, r12))
    scan2 = AdjointScan(z, head, -1, (src2, near2, out2, in2, s21, r21, s22, r22))
    ynear = [ypeers[d - 1] for d in sorted({d % NY for d in (1, -1, 2, -2)} - {0})]
    for off in range(1, ARC):
        pl.semaphore_signal(barrier, inc=1, device_id=(scan1.mate(off), head), device_id_type=MESH)

    for g in range(1, NZ // ARC):
        @pl.when(scan1.there(g))
        def _():
            pl.semaphore_signal(barrier, inc=1, device_id=((z + ARC * g) % NZ, head), device_id_type=MESH)

    for to in xpeers + ynear:
        pl.semaphore_signal(barrier, inc=1, device_id=(z, to), device_id_type=MESH)

    def products():
        loads[0].wait()
        loads[1].wait()
        total = jnp.zeros((HEAD_DIM, HEAD_DIM), F32)
        for n in range(blocks):
            vt[n] = v[n].T
            kvt[n] = total
            total = total + dot(vt[n], k[n])
        src1[...] = total.reshape(ARC, ROWS, HEAD_DIM)

    pl.when(z < NZ - 1)(products)
    pl.semaphore_wait(barrier, z // ARC + (ARC - 1 + len(xpeers) + len(ynear)))
    for g in range(1, NZ // ARC):
        @pl.when(scan2.there(g))
        def _():
            pl.semaphore_signal(greet.at[g], inc=1, device_id=((z + NZ - ARC * g) % NZ, head), device_id_type=MESH)

    pl.when(z == NZ - 1)(products)
    scan1.start()
    if NY > 5:
        for d in (2, NY - 2):
            pl.semaphore_signal(greet.at[0], inc=1, device_id=(z, ypeers[d - 1]), device_id_type=MESH)

    row = lax.broadcasted_iota(jnp.int32, (GROUP, GROUP), 0)
    col = lax.broadcasted_iota(jnp.int32, (GROUP, GROUP), 1)
    keep = row <= col
    loads[4].wait()
    gain = gain_ref[...]

    def local_scores(n):
        sct[n] = jnp.where(keep, dot_nt(k[n], q[n]), 0.0).astype(BF16)
        at[n] = dot(vt[n], sct[n])

    def local_rest(n):
        ut[n] = (og[n].astype(F32) * gain).T
        kt[n] = k[n].T

    loads[2].wait()
    loads[3].wait()
    for n in range(blocks):
        local_scores(n)
    for n in range(blocks):
        local_rest(n)
    scan1.pass_on(greet)
    scan1.share()
    scan1.finish(ext)

    tiles = GROUP // HEAD_DIM
    earlier = ext[...].reshape(HEAD_DIM, HEAD_DIM)
    xcopies, ycopies = {}, {}
    for n in range(blocks):
        state = earlier + kvt[n]
        st[n] = state
        hi, lo = split(state)
        a = at[n] + dot_nt(hi, q[n]) + dot_nt(lo, q[n])
        at[n] = a
        power = jnp.sum(a * a, axis=0, keepdims=True)
        cross = jnp.sum(a * ut[n], axis=0, keepdims=True)
        for c in range(tiles):
            stat[n, c : c + 1, :] = power[:, c * HEAD_DIM : (c + 1) * HEAD_DIM]
            stat[n, tiles + c : tiles + c + 1, :] = cross[:, c * HEAD_DIM : (c + 1) * HEAD_DIM]
        for d in sorted(range(1, NM), key=lambda d: -min(d, NM - d)):
            copy = pltpu.make_async_remote_copy(
                src_ref=stat.at[n], dst_ref=xin.at[n, d - 1],
                send_sem=sx.at[n, d - 1], recv_sem=rx.at[n, d - 1],
                device_id=(z, xpeers[d - 1]), device_id_type=MESH)
            copy.start()
            xcopies[n, d] = copy
    if NY > 5:
        pl.semaphore_wait(greet.at[0], 2)
    for n in range(blocks):
        total = stat[n]
        for d in range(1, NM):
            xcopies[n, d].wait()
            total = total + xin[n, d - 1]
        mstat[n] = total
        for d in sorted(range(1, NY), key=lambda d: -min(d, NY - d)):
            copy = pltpu.make_async_remote_copy(
                src_ref=mstat.at[n], dst_ref=yin.at[n, d - 1],
                send_sem=sy.at[n, d - 1], recv_sem=ry.at[n, d - 1],
                device_id=(z, ypeers[d - 1]), device_id_type=MESH)
            copy.start()
            ycopies[n, d] = copy
    for n in range(blocks):
        stdh[n], stdl[n] = split(st[n].T)
    suffix = jnp.zeros((HEAD_DIM, HEAD_DIM), F32)
    for n in range(blocks):
        total = mstat[n]
        for d in range(1, NY):
            ycopies[n, d].wait()
            total = total + yin[n, d - 1]
        ratio = lax.rsqrt(total[:tiles] / width + 1e-06)
        scale = ratio * ratio * ratio * (total[tiles:] / width)
        for c in range(tiles):
            part = slice(c * HEAD_DIM, (c + 1) * HEAD_DIM)
            agt[n, :, part] = (ratio[c : c + 1] * ut[n, :, part] - at[n, :, part] * scale[c : c + 1]).astype(BF16)
        adj[n] = dot(agt[n], q[n])
    for n in reversed(range(blocks)):
        own = adj[n]
        adj[n] = suffix
        suffix = suffix + own
    src2[...] = suffix.reshape(ARC, ROWS, HEAD_DIM)
    scan2.start()

    def local_grads(n):
        bft = jnp.where(keep, dot(v[n], agt[n]), 0.0).astype(BF16)
        qgt = dot(kt[n], bft) + dot(stdh[n], agt[n]) + dot(stdl[n], agt[n])
        qg[n] = qgt.T.astype(BF16)
        kgf[n] = dot(bft, q[n])
        ag[n] = agt[n].T
        vgf[n] = dot(sct[n], ag[n])

    for n in range(blocks // 2):
        local_grads(n)
    mine = scan2.gather()
    for g in reversed(range(NZ // ARC)):
        scan2.spread(g, mine)
    for n in range(blocks // 2, blocks):
        local_grads(n)
    scan2.finish(ext)
    later = ext[...].reshape(HEAD_DIM, HEAD_DIM)
    for n in range(blocks):
        adjh[n], adjl[n] = split(later + adj[n])
    scan1.close()
    scan2.close()


def finish(blocks, qg, kgf, vgf, k, v, adjh, adjl, qg_hbm, kg_hbm, vg_hbm, kg, vg, sem):
    copies = [pltpu.make_async_copy(qg, qg_hbm, sem.at[0, blocks])]
    copies[0].start()
    for n in range(blocks):
        hi, lo = adjh[n], adjl[n]
        kg[n] = (kgf[n] + dot(v[n], hi) + dot(v[n], lo)).astype(BF16)
        copies.append(pltpu.make_async_copy(kg.at[n], kg_hbm.at[n], sem.at[0, n]))
        copies[-1].start()
        vg[n] = (vgf[n] + dot_nt(k[n], hi) + dot_nt(k[n], lo)).astype(BF16)
        copies.append(pltpu.make_async_copy(vg.at[n], vg_hbm.at[n], sem.at[1, n]))
        copies[-1].start()
    for copy in copies:
        copy.wait()


def per_device(queries, keys, values, norm_gain, out_grad):
    tokens = queries.shape[0]
    blocks = tokens // GROUP
    width = lax.axis_size("head") * HEAD_DIM
    nat = (blocks, GROUP, HEAD_DIM)
    tra = (blocks, HEAD_DIM, GROUP)
    sq = (blocks, HEAD_DIM, HEAD_DIM)
    V = pltpu.VMEM
    D = pltpu.SemaphoreType.DMA
    piece = (ROWS, HEAD_DIM)
    srows = 2 * GROUP // HEAD_DIM
    zbuf = [V((ARC, *piece), F32), V((ARC - 1, *piece), F32), V((NZ, *piece), F32), V((NZ, *piece), F32)]
    zsem = [D((ARC - 1,)), D((ARC - 1,)), D((NZ,)), D((NZ,))]
    anyspec = pl.BlockSpec(memory_space=pl.ANY)
    hbmspec = pl.BlockSpec(memory_space=pltpu.HBM)
    vspec = pl.BlockSpec(memory_space=pltpu.VMEM)
    out = pl.pallas_call(
        lambda *refs: kernel(blocks, width, *refs),
        out_shape=[KEPT(nat, BF16), KEPT(nat, F32), KEPT(nat, F32), KEPT(nat, BF16), KEPT(nat, BF16),
                   KEPT(sq, BF16), KEPT(sq, BF16)],
        in_specs=[hbmspec] * 5,
        out_specs=[vspec] * 7,
        scratch_shapes=[V(nat, BF16)] * 2
        + [V((1, HEAD_DIM), F32), V(tra, BF16), V(tra, BF16), V(tra, F32), V(tra, F32), V((blocks, GROUP, GROUP), BF16),
           V(tra, BF16), V(nat, BF16),
           V(sq, F32), V(sq, F32), V(sq, BF16), V(sq, BF16), V(sq, F32),
           V((ARC, *piece), F32)]
        + zbuf + zbuf
        + [V((blocks, srows, HEAD_DIM), F32), V((blocks, srows, HEAD_DIM), F32),
           V((blocks, NM - 1, srows, HEAD_DIM), F32), V((blocks, NY - 1, srows, HEAD_DIM), F32)]
        + [D((5,)), pltpu.SemaphoreType.REGULAR((NZ // ARC,))] + zsem + zsem
        + [D((blocks, NM - 1))] * 2 + [D((blocks, NY - 1))] * 2,
        compiler_params=pltpu.CompilerParams(collective_id=0, has_side_effects=True, vmem_limit_bytes=VMEM_LIMIT),
        name="attention_backward",
    )(*(pltpu.with_memory_space_constraint(a.reshape(nat), pltpu.HBM) for a in (queries, keys, values)),
      pltpu.with_memory_space_constraint(norm_gain.reshape(1, HEAD_DIM), pltpu.HBM),
      pltpu.with_memory_space_constraint(out_grad.reshape(nat), pltpu.HBM))
    out = pl.pallas_call(
        lambda *refs: finish(blocks, *refs),
        out_shape=[jax.ShapeDtypeStruct(nat, BF16)] * 3,
        in_specs=[vspec] * 7,
        out_specs=[anyspec] * 3,
        scratch_shapes=[V(nat, BF16)] * 2 + [D((2, blocks + 1))],
        compiler_params=pltpu.CompilerParams(vmem_limit_bytes=VMEM_LIMIT // 4),
        name="finish",
    )(*(pltpu.with_memory_space_constraint(o, pltpu.VMEM) for o in out))
    return tuple(o.reshape(tokens, HEAD_DIM) for o in out)


def solution(mesh):
    return jax.shard_map(
        per_device,
        mesh=mesh,
        in_specs=(
            P("ctx", "head"),
            P("ctx", "head"),
            P("ctx", "head"),
            P("head"),
            P("ctx", "head"),
        ),
        out_specs=(P("ctx", "head"), P("ctx", "head"), P("ctx", "head")),
        check_vma=False,
    )
```
